32 devices in a mesh: dp: 8 (over y, x, core), mp: 4 (over z).
Axes of the slice: x: 2, y: 2, z: 4, core: 2. Of those that a mesh axis runs over, the one named last changes fastest.
Arguments:
- activations: bfloat16 [1024, 2560], P('dp'), may hold values from -6 to 6
- grad_hidden: bfloat16 [1024, 8192], P('dp', 'mp'), may hold values from -0.059814453 to 0.059814453
- up_weight: bfloat16 [2560, 8192], P('dp', 'mp'), may hold values from -6 to 6
- error_feedback: bfloat16 [8, 2560, 8192], P('dp', None, 'mp'), may hold values from -0.75 to 0.75
- query_previous: float32 [8192, 128], P('mp'), may hold values from -6 to 6
Outputs:
- grad_input: bfloat16 [1024, 2560], P('dp', 'mp')
- error_next: bfloat16 [8, 2560, 8192], P('dp', None, 'mp')
- update: float32 [2560, 8192], P('dp', 'mp')
- query_next: float32 [8192, 128], P('mp')
The draws below stay inside these ranges and needn't reach their ends.
All inputs are finite; a program needn't handle non-finite values.
Results may differ from the reference program's by a relative error of at most 0.0005.
Values may be sent and summed in bfloat16 or wider, within the bound.
A program may use at most 128 MiB of HBM per device.

```python
import jax
import jax.numpy as jnp
from jax import lax

D = 2560
FF = 8192
R = 128
TOK_DEV = 128
TOKENS = 1024
N_DP = 8


def with_spikes(drawn, key, source, target, blocks, factor):
    def block_of(position):
        return (jnp.arange(drawn.shape[position]) // (drawn.shape[position] // blocks)).reshape((-1,) + (1,) * (drawn.ndim - 1 - position))

    near = jax.random.permutation(key, blocks)[block_of(target)]
    second = (block_of(target) + blocks // 2) % blocks
    return jnp.where((block_of(source) == near) | (block_of(source) == second), factor * drawn, drawn)


def level_of(rng, dims, split, smallest, largest):
    gain = 1.0
    for axis_at, blocks in split:
        draws = jax.random.uniform(jax.random.fold_in(jax.random.fold_in(rng, 6), axis_at), (blocks,), jnp.float32, smallest / len(split), largest / len(split))
        gain = gain * jnp.repeat(jnp.exp(draws), dims[axis_at] // blocks).reshape((-1,) + (1,) * (len(dims) - 1 - axis_at))
    return gain


def scatter_about(stream_key, extent, deviation, reach, split=(), kind=jnp.bfloat16):
    entries = jax.random.normal(stream_key, extent, jnp.float32) * deviation
    if len(split) > 0:
        entries = level_of(stream_key, extent, split, -0.22, 0.18) * entries
    return jnp.clip(entries, min=-reach, max=reach).astype(kind)


def noise_with(own_key, dims, scale, limit, shards, heavy, kind=jnp.bfloat16):
    result = scale * jax.random.normal(own_key, dims, jnp.float32)
    if shards:
        result = result * level_of(own_key, dims, shards, -0.22, 0.18)
    return jnp.clip(with_spikes(result, jax.random.fold_in(own_key, 3), *heavy), -limit, limit).astype(kind)


def setup_inputs(seed: int = 0) -> dict:
    arg_keys = jax.random.split(jax.random.key(seed), 6)
    return {
        "activations": noise_with(arg_keys[0], (TOKENS, D), 1.0, 6.0, ((0, 8),), (0, 1, 8, 2.0)),
        "grad_hidden": scatter_about(arg_keys[1], (TOKENS, FF), 0.01, 0.059814453, ((0, 8), (1, 4))),
        "up_weight": scatter_about(arg_keys[2], (D, FF), 1.0, 6.0, ((0, 8), (1, 4))),
        "error_feedback": scatter_about(arg_keys[3], (N_DP, D, FF), 0.125, 0.75, ((0, 8), (2, 4))),
        "query_previous": scatter_about(arg_keys[4], (FF, R), 1.0, 6.0, ((0, 4),), jnp.float32),
    }


HIGHEST = lax.Precision.HIGHEST

def merged_of(error_block, acts_block, hidden_block):
    return error_block.astype(jnp.float32) + jnp.dot(acts_block.T.astype(jnp.float32), hidden_block.astype(jnp.float32), preferred_element_type=jnp.float32)

def reference(activations, grad_hidden, up_weight, error_feedback, query_previous):
    grad_input = jnp.dot(grad_hidden.astype(jnp.float32), up_weight.T.astype(jnp.float32), preferred_element_type=jnp.float32).astype(jnp.bfloat16)
    acts_split = activations.reshape(N_DP, TOK_DEV, D)
    hidden_split = grad_hidden.reshape(N_DP, TOK_DEV, FF)
    stacked = (error_feedback, acts_split, hidden_split)

    def add_project(running, inputs):
        merged = merged_of(inputs[0], inputs[1], inputs[2])
        return (running + jnp.dot(merged.astype(jnp.float32), query_previous.astype(jnp.float32), precision=HIGHEST, preferred_element_type=jnp.float32), None)
    project, unused = lax.scan(add_project, jnp.zeros((D, R), jnp.float32), stacked)
    gram_matrix = jnp.dot(project.T.astype(jnp.float32), project.astype(jnp.float32), precision=HIGHEST, preferred_element_type=jnp.float32)
    factor = jnp.linalg.cholesky(gram_matrix)
    basis = lax.linalg.triangular_solve(factor, project, left_side=False, lower=True, transpose_a=True)

    def add_query(running, inputs):
        merged = merged_of(inputs[0], inputs[1], inputs[2])
        return (running + jnp.dot(merged.T.astype(jnp.float32), basis.astype(jnp.float32), precision=HIGHEST, preferred_element_type=jnp.float32), None)
    query_total, unused = lax.scan(add_query, jnp.zeros((FF, R), jnp.float32), stacked)
    query_next = query_total / N_DP
    update = jnp.dot(basis.astype(jnp.float32), query_next.T.astype(jnp.float32), precision=HIGHEST, preferred_element_type=jnp.float32)

    def residual_of(inputs):
        return (merged_of(inputs[0], inputs[1], inputs[2]) - update).astype(jnp.bfloat16)
    error_next = lax.map(residual_of, stacked)
    return (grad_input, error_next, update, query_next)
```

```python
import functools

import jax
import jax.numpy as jnp
from jax import lax
from jax.experimental import pallas as pl
from jax.experimental.pallas import tpu as pltpu
from jax.sharding import PartitionSpec as P

HIGHEST = lax.Precision.HIGHEST
MESH = pl.DeviceIdType.MESH
F32 = jnp.float32
BF16 = jnp.bfloat16
CORES = 2
PANEL = 16


def split(x):
    high = x.astype(BF16)
    return high, (x - high.astype(F32)).astype(BF16)


def dot(a, b, da=1, db=0, precision=None):
    return lax.dot_general(
        a, b, (((da,), (db,)), ((), ())), precision=precision, preferred_element_type=F32
    )


def halves(x):
    r = x.shape[1] // 2
    return x[:, :r] + x[:, r:]


def inverse_factor(gram, aug):
    r = gram.shape[0]
    rows = lax.broadcasted_iota(jnp.int32, (r, r), 0)
    cols = lax.broadcasted_iota(jnp.int32, (r, r), 1)
    aug[:, :r] = gram
    aug[:, r:] = jnp.where(rows == cols, 1.0, 0.0).astype(F32)
    prow = lax.broadcasted_iota(jnp.int32, (PANEL, 2 * r), 0)
    for start in range(0, r, PANEL):
        panel = aug[start : start + PANEL, :]
        for t in range(PANEL):
            j = start + t
            scale = lax.rsqrt(panel[t : t + 1, j : j + 1])
            row = panel[t : t + 1, :] * scale
            col = panel[:, j : j + 1] * scale
            panel = jnp.where(
                prow == t, row, jnp.where(prow > t, panel - col * row, panel)
            )
        aug[start : start + PANEL, :] = panel
        rest = start + PANEL
        if rest < r:
            change = dot(panel[:, :r], panel, 0, 0, HIGHEST)
            aug[rest:, :] = aug[rest:, :] - change[rest:, :]
    return aug[:, r:]


def compress(
    n_dp, n_mp, e_hbm, a_ref, h_hbm, h_ref, q_ref, qn_ref, b_ref,
    e, q2, p, pt2, aug, acc, zin, zfin, csend, crecv, xsend, xrecv,
    t, tcrecv, txsend, txrecv,
    e_sem, c_s, c_r, x_s, x_r, z_s, z_r, gz_s, gz_r, gx_s, gx_r, gc_s, gc_r,
    tc_s, tc_r, tx_s, tx_r, qx_s, qx_r, qc_s, qc_r,
):
    chips = n_dp // CORES
    me, mp = lax.axis_index("dp"), lax.axis_index("mp")
    chip, core = me // CORES, lax.rem(me, CORES)
    other = 1 - core
    partner = (chip * CORES + other, mp)
    d, rank = p.shape
    ff = t.shape[0]
    pr, tr = d // n_dp, ff // n_dp
    zr = pr // n_mp if pr % (8 * n_mp) == 0 else pr

    def chip_at(r):
        return lax.rem(chip + r, chips)

    def same_core(r):
        return (chip_at(r) * CORES + core, mp)

    def along(r):
        return (me, lax.rem(mp + r, n_mp))

    def rows(i, n):
        return pl.ds(pl.multiple_of(i * n, 8), n)

    def send(src, dst, s, r, to):
        return pltpu.make_async_remote_copy(
            src_ref=src, dst_ref=dst, send_sem=s, recv_sem=r, device_id=to, device_id_type=MESH
        )

    barrier = pltpu.get_barrier_semaphore()
    pl.semaphore_signal(barrier, inc=1, device_id=partner, device_id_type=MESH)
    for r in range(1, chips):
        pl.semaphore_signal(barrier, inc=1, device_id=same_core(r), device_id_type=MESH)
    for r in range(1, n_mp):
        pl.semaphore_signal(barrier, inc=1, device_id=along(r), device_id_type=MESH)

    order = [chip_at(r) * CORES + other for r in range(1, chips)] + [partner[0]]
    order += [chip_at(r) * CORES + core for r in range(1, chips)] + [me]
    loads = []
    for i, block in enumerate(order):
        at = pl.ds(pl.multiple_of(block * pr, 16), pr)
        copy = pltpu.make_async_copy(e_hbm.at[at, :], e.at[at, :], e_sem.at[i])
        copy.start()
        loads.append(copy)
    h_load = pltpu.make_async_copy(h_hbm, e.at[pl.ds(d, h_ref.shape[0]), :], e_sem.at[n_dp])
    h_load.start()

    q_high, q_low = split(q_ref[...])
    q2[:, :rank] = q_high
    q2[:, rank:] = q_low
    hq = halves(dot(h_ref[...], q2[...]))
    hq2 = jnp.concatenate(split(hq), axis=1)
    p[...] = halves(dot(a_ref[...], hq2, 0, 0))

    def project(i):
        loads[i].wait()
        block = order[i]
        at = pl.ds(pl.multiple_of(block * pr, 16), pr)
        return halves(dot(e[at, :], q2[...])) + p[rows(block, pr), :]

    pl.semaphore_wait(barrier, 1 + (chips - 1) + (n_mp - 1))
    core_copies = []
    for i in range(chips):
        csend[i] = project(i)
        copy = send(csend.at[i], crecv.at[i], c_s.at[i], c_r.at[i], partner)
        copy.start()
        core_copies.append(copy)
    x_copies = []
    for i in range(chips):
        value = project(chips + i)
        core_copies[i].wait_recv()
        value = value + crecv[i]
        if i < chips - 1:
            xsend[i] = value
            copy = send(xsend.at[i], xrecv.at[i], x_s.at[i], x_r.at[i], same_core(i + 1))
            copy.start()
            x_copies.append(copy)
        else:
            acc[...] = value
    h_load.wait()
    value = acc[...]
    for i, copy in enumerate(x_copies):
        copy.wait_recv()
        value = value + xrecv[i]
    acc[...] = value

    def part(i):
        return rows(i, zr) if zr < pr else pl.ds(0, pr)

    z_copies = []
    for r in range(1, n_mp):
        copy = send(
            acc.at[part(lax.rem(mp + r, n_mp)), :], zin.at[r - 1], z_s.at[r - 1], z_r.at[r - 1], along(r)
        )
        copy.start()
        z_copies.append(copy)
    value = acc[part(mp), :]
    for i, copy in enumerate(z_copies):
        copy.wait_recv()
        value = value + zin[i]
    mine = pl.ds(pl.multiple_of(me * pr, 8), pr)
    if zr < pr:
        zfin[...] = value
        here = pl.ds(pl.multiple_of(me * pr + mp * zr, 8), zr)
        p[here, :] = value
        gz = []
        for r in range(1, n_mp):
            copy = send(zfin, p.at[here, :], gz_s.at[r - 1], gz_r.at[r - 1], along(r))
            copy.start()
            gz.append(copy)
        for r in range(1, n_mp):
            gz[r - 1].wait_recv()
        z_copies += gz
    else:
        p[mine, :] = value

    def gather(ref, n, x_s, x_r, c_s, c_r, between=None):
        own = pl.ds(pl.multiple_of(me * n, 8), n)
        across, down = [], []
        for r in range(1, chips):
            copy = send(ref.at[own, :], ref.at[own, :], x_s.at[r - 1], x_r.at[r - 1], same_core(r))
            copy.start()
            across.append(copy)
        copy = send(ref.at[own, :], ref.at[own, :], c_s.at[chips - 1], c_r.at[chips - 1], partner)
        copy.start()
        down.append(copy)
        if between is not None:
            between()
        for r in range(1, chips):
            across[r - 1].wait_recv()
            block = lax.rem(chip + chips - r, chips) * CORES + core
            at = pl.ds(pl.multiple_of(block * n, 8), n)
            copy = send(ref.at[at, :], ref.at[at, :], c_s.at[r - 1], c_r.at[r - 1], partner)
            copy.start()
            down.append(copy)
        for copy in down:
            copy.wait_recv()
        return across + down

    started = core_copies + x_copies
    for copy in started:
        copy.wait_send()
    for copy in z_copies:
        copy.wait_send()
    for copy in gather(p, pr, gx_s, gx_r, gc_s, gc_r):
        copy.wait_send()

    pt = p[...].T
    high, low = split(pt)
    pt2[:rank, :d] = high
    pt2[rank:, :d] = low
    ap = dot(pt2[:, :d], a_ref[...], 1, 1)
    high, low = split(ap[:rank] + ap[rank:])
    pt2[:rank, d:] = high
    pt2[rank:, d:] = low
    width = 256

    def term(n, carry):
        at = pl.ds(pl.multiple_of(n * width, width), width)
        both = dot(pt2[...], e[:, at])
        t[at, :] = (both[:rank] + both[rank:]).T
        return carry

    lax.fori_loop(0, ff // width, term, 0)
    t_copies = []
    for i in range(chips):
        block = chip_at(i + 1) * CORES + other
        copy = send(t.at[rows(block, tr), :], tcrecv.at[i], tc_s.at[i], tc_r.at[i], partner)
        copy.start()
        t_copies.append(copy)
    gram = dot(pt, p[...], 1, 0, HIGHEST)
    tx_copies = []
    for i in range(chips):
        t_copies[i].wait_recv()
        value = t[rows(chip_at(i + 1) * CORES + core, tr), :] + tcrecv[i]
        txsend[i] = value
        if i < chips - 1:
            copy = send(txsend.at[i], txrecv.at[i], tx_s.at[i], tx_r.at[i], same_core(i + 1))
            copy.start()
            tx_copies.append(copy)
    inverse = inverse_factor(gram, aug)
    value = txsend[chips - 1]
    for i, copy in enumerate(tx_copies):
        copy.wait_recv()
        value = value + txrecv[i]
    for copy in t_copies + tx_copies:
        copy.wait_send()
    qn_ref[rows(me, tr), :] = dot(value, inverse, 1, 1, HIGHEST) / n_dp

    def basis():
        high, low = split(dot(p[...], aug[:, rank:], 1, 1, HIGHEST))
        b_ref[:, :rank] = high
        b_ref[:, rank:] = low

    for copy in gather(qn_ref, tr, qx_s, qx_r, qc_s, qc_r, basis):
        copy.wait_send()


def residual(n_dp, e_ref, a_ref, h_ref, qn_ref, b_ref, out_ref, up_ref, y):
    tok, rank = h_ref.shape[0], qn_ref.shape[1]
    rows = e_ref.shape[0]
    step = pl.program_id(0)

    @pl.when(step == 0)
    def _():
        high, low = split(-qn_ref[...].T)
        y[:rank] = high
        y[rank : 2 * rank] = high
        y[2 * rank : 3 * rank] = low
        y[3 * rank :] = h_ref[...]
        share = up_ref.shape[0]
        own = b_ref[pl.ds(pl.multiple_of(lax.axis_index("dp") * share, 16), share), :]
        x = jnp.concatenate([own, own[:, :rank]], axis=1)
        up_ref[...] = -dot(x, y[: 3 * rank, :])

    b = b_ref[pl.ds(pl.multiple_of(step * rows, 16), rows), :]
    x = jnp.concatenate([b, b[:, :rank], a_ref[...].T], axis=1)
    out_ref[...] = (e_ref[...].astype(F32) + dot(x, y[...])).astype(BF16)


def local(n_dp, n_mp, activations, grad_hidden, up_weight, error_feedback, query_previous):
    error = error_feedback[0]
    d, ff = error.shape
    tok, rank = activations.shape[0], query_previous.shape[1]
    partial_input = lax.dot_general(
        grad_hidden,
        lax.all_gather(up_weight, "dp", axis=0, tiled=True),
        (((1,), (1,)), ((), ())),
        preferred_element_type=F32,
    )
    grad_input = lax.psum_scatter(partial_input, "mp", scatter_dimension=1, tiled=True).astype(BF16)

    chips = n_dp // CORES
    pr, tr = d // n_dp, ff // n_dp
    zr = pr // n_mp if pr % (8 * n_mp) == 0 else pr
    vmem = pl.BlockSpec(memory_space=pltpu.VMEM)
    hbm = pl.BlockSpec(memory_space=pl.ANY)
    dma = pltpu.SemaphoreType.DMA
    pairs = lambda n: [dma((n,)), dma((n,))]
    query_next, basis = pl.pallas_call(
        functools.partial(compress, n_dp, n_mp),
        out_shape=(
            jax.ShapeDtypeStruct((ff, rank), F32),
            jax.ShapeDtypeStruct((d, 2 * rank), BF16),
        ),
        in_specs=[hbm, vmem, hbm, vmem, vmem],
        out_specs=(vmem, vmem),
        scratch_shapes=[
            pltpu.VMEM((d + tok, ff), BF16),
            pltpu.VMEM((ff, 2 * rank), BF16),
            pltpu.VMEM((d, rank), F32),
            pltpu.VMEM((2 * rank, d + tok), BF16),
            pltpu.VMEM((rank, 2 * rank), F32),
            pltpu.VMEM((pr, rank), F32),
            pltpu.VMEM((n_mp, zr, rank), F32),
            pltpu.VMEM((zr, rank), F32),
            pltpu.VMEM((chips, pr, rank), F32),
            pltpu.VMEM((chips, pr, rank), F32),
            pltpu.VMEM((chips, pr, rank), F32),
            pltpu.VMEM((chips, pr, rank), F32),
            pltpu.VMEM((ff, rank), F32),
            pltpu.VMEM((chips, tr, rank), F32),
            pltpu.VMEM((chips, tr, rank), F32),
            pltpu.VMEM((chips, tr, rank), F32),
            dma((n_dp + 1,)),
        ]
        + pairs(chips) + pairs(chips) + pairs(n_mp) + pairs(n_mp) + pairs(chips) + pairs(chips)
        + pairs(chips) + pairs(chips) + pairs(chips) + pairs(chips),
        compiler_params=pltpu.CompilerParams(
            collective_id=0, has_side_effects=True, vmem_limit_bytes=48 << 20
        ),
        cost_estimate=pl.CostEstimate(flops=8 * d * ff * rank, bytes_accessed=4 * d * ff, transcendentals=0),
        name="compress",
    )(error, activations, grad_hidden, grad_hidden, query_previous)

    block = 256
    error_next, update = pl.pallas_call(
        functools.partial(residual, n_dp),
        out_shape=(
            jax.ShapeDtypeStruct((d, ff), BF16),
            jax.ShapeDtypeStruct((pr, ff), F32),
        ),
        grid=(d // block,),
        in_specs=[
            pl.BlockSpec((block, ff), lambda i: (i, 0)),
            pl.BlockSpec((tok, block), lambda i: (0, i)),
            pl.BlockSpec((tok, ff), lambda i: (0, 0)),
            pl.BlockSpec((ff, rank), lambda i: (0, 0)),
            pl.BlockSpec((d, 2 * rank), lambda i: (0, 0)),
        ],
        out_specs=(
            pl.BlockSpec((block, ff), lambda i: (i, 0)),
            pl.BlockSpec((pr, ff), lambda i: (0, 0)),
        ),
        scratch_shapes=[pltpu.VMEM((3 * rank + tok, ff), BF16)],
        compiler_params=pltpu.CompilerParams(vmem_limit_bytes=40 << 20),
        cost_estimate=pl.CostEstimate(flops=8 * d * ff * rank, bytes_accessed=4 * d * ff, transcendentals=0),
        name="residual",
    )(error, activations, grad_hidden, query_next, basis)
    return grad_input, error_next[None], update, query_next


def solution(mesh):
    n_dp, n_mp = mesh.shape["dp"], mesh.shape["mp"]
    in_specs = (P("dp", None), P("dp", "mp"), P("dp", "mp"), P("dp", None, "mp"), P("mp", None))
    out_specs = (P("dp", "mp"), P("dp", None, "mp"), P("dp", "mp"), P("mp", None))
    return jax.shard_map(
        functools.partial(local, n_dp, n_mp),
        mesh=mesh, in_specs=in_specs, out_specs=out_specs, check_vma=False,
    )
```

```python
import functools

import jax
import jax.numpy as jnp
from jax import lax
from jax.experimental import pallas as pl
from jax.experimental.pallas import tpu as pltpu
from jax.sharding import PartitionSpec as P

HIGHEST = lax.Precision.HIGHEST
MESH = pl.DeviceIdType.MESH
F32 = jnp.float32
BF16 = jnp.bfloat16
CORES = 2
PANEL = 16


def split(x):
    high = x.astype(BF16)
    return high, (x - high.astype(F32)).astype(BF16)


def dot(a, b, da=1, db=0, precision=None):
    return lax.dot_general(
        a, b, (((da,), (db,)), ((), ())), precision=precision, preferred_element_type=F32
    )


def halves(x):
    r = x.shape[1] // 2
    return x[:, :r] + x[:, r:]


def inverse_factor(gram, aug):
    r = gram.shape[0]
    rows = lax.broadcasted_iota(jnp.int32, (r, r), 0)
    cols = lax.broadcasted_iota(jnp.int32, (r, r), 1)
    aug[:, :r] = gram
    aug[:, r:] = jnp.where(rows == cols, 1.0, 0.0).astype(F32)
    prow = lax.broadcasted_iota(jnp.int32, (PANEL, 2 * r), 0)
    for start in range(0, r, PANEL):
        panel = aug[start : start + PANEL, :]
        for t in range(PANEL):
            j = start + t
            scale = lax.rsqrt(panel[t : t + 1, j : j + 1])
            row = panel[t : t + 1, :] * scale
            col = panel[:, j : j + 1] * scale
            panel = jnp.where(
                prow == t, row, jnp.where(prow > t, panel - col * row, panel)
            )
        aug[start : start + PANEL, :] = panel
        rest = start + PANEL
        if rest < r:
            change = dot(panel[:, :r], panel, 0, 0, HIGHEST)
            aug[rest:, :] = aug[rest:, :] - change[rest:, :]
    return aug[:, r:]


def compress(
    n_dp, n_mp, e_hbm, a_ref, h_hbm, h_ref, q_ref, w_ref, qn_ref, b_ref, gi_ref,
    e, q2, p, pt2, aug, acc, zin, zfin, csend, crecv, xsend, xrecv,
    t, tcrecv, txsend, txrecv, hall, gsend, grecv,
    e_sem, c_s, c_r, x_s, x_r, z_s, z_r, gz_s, gz_r, gx_s, gx_r, gc_s, gc_r,
    tc_s, tc_r, tx_s, tx_r, qx_s, qx_r, qc_s, qc_r,
    hx_s, hx_r, hc_s, hc_r, g_s, g_r,
):
    chips = n_dp // CORES
    me, mp = lax.axis_index("dp"), lax.axis_index("mp")
    chip, core = me // CORES, lax.rem(me, CORES)
    other = 1 - core
    partner = (chip * CORES + other, mp)
    d, rank = p.shape
    ff = t.shape[0]
    pr, tr = d // n_dp, ff // n_dp
    zr = pr // n_mp if pr % (8 * n_mp) == 0 else pr

    def chip_at(r):
        return lax.rem(chip + r, chips)

    def same_core(r):
        return (chip_at(r) * CORES + core, mp)

    def along(r):
        return (me, lax.rem(mp + r, n_mp))

    def rows(i, n):
        return pl.ds(pl.multiple_of(i * n, 8), n)

    def send(src, dst, s, r, to):
        return pltpu.make_async_remote_copy(
            src_ref=src, dst_ref=dst, send_sem=s, recv_sem=r, device_id=to, device_id_type=MESH
        )

    barrier = pltpu.get_barrier_semaphore()
    pl.semaphore_signal(barrier, inc=1, device_id=partner, device_id_type=MESH)
    for r in range(1, chips):
        pl.semaphore_signal(barrier, inc=1, device_id=same_core(r), device_id_type=MESH)
    for r in range(1, n_mp):
        pl.semaphore_signal(barrier, inc=1, device_id=along(r), device_id_type=MESH)

    group = n_dp // n_mp
    target = me // group
    for k in range(group):
        for m in range(n_mp):
            source = mp * group + k

            @pl.when(jnp.logical_or(source != me, mp != m))
            def _(source=source, m=m):
                pl.semaphore_signal(barrier, inc=1, device_id=(source, m), device_id_type=MESH)

    order = [chip_at(r) * CORES + other for r in range(1, chips)] + [partner[0]]
    order += [chip_at(r) * CORES + core for r in range(1, chips)] + [me]
    loads = []
    for i, block in enumerate(order):
        at = pl.ds(pl.multiple_of(block * pr, 16), pr)
        copy = pltpu.make_async_copy(e_hbm.at[at, :], e.at[at, :], e_sem.at[i])
        copy.start()
        loads.append(copy)
    h_load = pltpu.make_async_copy(h_hbm, e.at[pl.ds(d, h_ref.shape[0]), :], e_sem.at[n_dp])
    h_load.start()

    q_high, q_low = split(q_ref[...])
    q2[:, :rank] = q_high
    q2[:, rank:] = q_low
    hq = halves(dot(h_ref[...], q2[...]))
    hq2 = jnp.concatenate(split(hq), axis=1)
    p[...] = halves(dot(a_ref[...], hq2, 0, 0))

    def project(i):
        loads[i].wait()
        block = order[i]
        at = pl.ds(pl.multiple_of(block * pr, 16), pr)
        return halves(dot(e[at, :], q2[...])) + p[rows(block, pr), :]

    pl.semaphore_wait(barrier, chips + n_mp - 1 + n_dp - jnp.where(target == mp, 1, 0))
    core_copies = []
    for i in range(chips):
        csend[i] = project(i)
        copy = send(csend.at[i], crecv.at[i], c_s.at[i], c_r.at[i], partner)
        copy.start()
        core_copies.append(copy)
    x_copies = []
    for i in range(chips):
        value = project(chips + i)
        core_copies[i].wait_recv()
        value = value + crecv[i]
        if i < chips - 1:
            xsend[i] = value
            copy = send(xsend.at[i], xrecv.at[i], x_s.at[i], x_r.at[i], same_core(i + 1))
            copy.start()
            x_copies.append(copy)
        else:
            acc[...] = value
    h_across = [
        send(h_ref, hall.at[me], hx_s.at[r - 1], hx_r.at[r - 1], same_core(r)) for r in range(1, chips)
    ]
    early = min(2, chips - 1)
    for copy in h_across[:early]:
        copy.start()
    h_down = [send(h_ref, hall.at[me], hc_s.at[chips - 1], hc_r.at[chips - 1], partner)]
    h_down[0].start()

    def late_sends():
        for copy in h_across[early:]:
            copy.start()

    def pass_down(rs):
        for r in rs:
            h_across[r - 1].wait_recv()
            block = lax.rem(chip + chips - r, chips) * CORES + core
            copy = send(hall.at[block], hall.at[block], hc_s.at[r - 1], hc_r.at[r - 1], partner)
            copy.start()
            h_down.append(copy)

    h_load.wait()
    value = acc[...]
    for i, copy in enumerate(x_copies):
        copy.wait_recv()
        value = value + xrecv[i]
    acc[...] = value

    def part(i):
        return rows(i, zr) if zr < pr else pl.ds(0, pr)

    z_copies = []
    for r in range(1, n_mp):
        copy = send(
            acc.at[part(lax.rem(mp + r, n_mp)), :], zin.at[r - 1], z_s.at[r - 1], z_r.at[r - 1], along(r)
        )
        copy.start()
        z_copies.append(copy)
    value = acc[part(mp), :]
    for i, copy in enumerate(z_copies):
        copy.wait_recv()
        value = value + zin[i]
    mine = pl.ds(pl.multiple_of(me * pr, 8), pr)
    if zr < pr:
        zfin[...] = value
        here = pl.ds(pl.multiple_of(me * pr + mp * zr, 8), zr)
        p[here, :] = value
        gz = []
        for r in range(1, n_mp):
            copy = send(zfin, p.at[here, :], gz_s.at[r - 1], gz_r.at[r - 1], along(r))
            copy.start()
            gz.append(copy)
        for r in range(1, n_mp):
            gz[r - 1].wait_recv()
        z_copies += gz
    else:
        p[mine, :] = value

    def gather(ref, n, x_s, x_r, c_s, c_r, between=None):
        own = pl.ds(pl.multiple_of(me * n, 8), n)
        across, down = [], []
        for r in range(1, chips):
            copy = send(ref.at[own, :], ref.at[own, :], x_s.at[r - 1], x_r.at[r - 1], same_core(r))
            copy.start()
            across.append(copy)
        copy = send(ref.at[own, :], ref.at[own, :], c_s.at[chips - 1], c_r.at[chips - 1], partner)
        copy.start()
        down.append(copy)
        if between is not None:
            between()
        for r in range(1, chips):
            across[r - 1].wait_recv()
            block = lax.rem(chip + chips - r, chips) * CORES + core
            at = pl.ds(pl.multiple_of(block * n, 8), n)
            copy = send(ref.at[at, :], ref.at[at, :], c_s.at[r - 1], c_r.at[r - 1], partner)
            copy.start()
            down.append(copy)
        for copy in down:
            copy.wait_recv()
        return across + down

    started = core_copies + x_copies
    for copy in started:
        copy.wait_send()
    for copy in z_copies:
        copy.wait_send()
    for copy in gather(p, pr, gx_s, gx_r, gc_s, gc_r, late_sends):
        copy.wait_send()
    pass_down(range(1, early + 1))

    pt = p[...].T
    high, low = split(pt)
    pt2[:rank, :d] = high
    pt2[rank:, :d] = low
    ap = dot(pt2[:, :d], a_ref[...], 1, 1)
    high, low = split(ap[:rank] + ap[rank:])
    pt2[:rank, d:] = high
    pt2[rank:, d:] = low
    width = 256

    def term(n, carry):
        at = pl.ds(pl.multiple_of(n * width, width), width)
        both = dot(pt2[...], e[:, at])
        t[at, :] = (both[:rank] + both[rank:]).T
        return carry

    lax.fori_loop(0, ff // width, term, 0)
    t_copies = []
    for i in range(chips):
        block = chip_at(i + 1) * CORES + other
        copy = send(t.at[rows(block, tr), :], tcrecv.at[i], tc_s.at[i], tc_r.at[i], partner)
        copy.start()
        t_copies.append(copy)
    gram = dot(pt, p[...], 1, 0, HIGHEST)
    tx_copies = []
    for i in range(chips):
        t_copies[i].wait_recv()
        value = t[rows(chip_at(i + 1) * CORES + core, tr), :] + tcrecv[i]
        txsend[i] = value
        if i < chips - 1:
            copy = send(txsend.at[i], txrecv.at[i], tx_s.at[i], tx_r.at[i], same_core(i + 1))
            copy.start()
            tx_copies.append(copy)
    pass_down(range(early + 1, chips))
    for copy in h_down:
        copy.wait_recv()

    slot = lax.rem(me, group) * n_mp + mp

    def outgoing(i):
        to = (lax.rem(me + i, n_dp), target)
        return send(gsend.at[i], grecv.at[slot], g_s.at[i], g_r.at[slot], to)

    def partial(i, carry):
        gsend[i] = dot(hall[lax.rem(me + i, n_dp)], w_ref[...], 1, 1)
        outgoing(i).start()
        return carry

    lax.fori_loop(1, n_dp, partial, 0)
    own_part = dot(h_ref[...], w_ref[...], 1, 1)

    @pl.when(target == mp)
    def _():
        grecv[slot] = own_part

    @pl.when(target != mp)
    def _():
        gsend[0] = own_part
        outgoing(0).start()

    inverse = inverse_factor(gram, aug)
    value = txsend[chips - 1]
    for i, copy in enumerate(tx_copies):
        copy.wait_recv()
        value = value + txrecv[i]
    for copy in t_copies + tx_copies:
        copy.wait_send()
    qn_ref[rows(me, tr), :] = dot(value, inverse, 1, 1, HIGHEST) / n_dp

    def basis():
        high, low = split(dot(p[...], aug[:, rank:], 1, 1, HIGHEST))
        b_ref[:, :rank] = high
        b_ref[:, rank:] = low

    for copy in gather(qn_ref, tr, qx_s, qx_r, qc_s, qc_r, basis):
        copy.wait_send()
    for k in range(group):
        for m in range(n_mp):
            i = k * n_mp + m

            @pl.when(jnp.logical_or(mp * group + k != me, mp != m))
            def _(i=i):
                send(gsend.at[i], grecv.at[i], g_s.at[i], g_r.at[i], partner).wait_recv()

        total = grecv[k * n_mp]
        for m in range(1, n_mp):
            total = total + grecv[k * n_mp + m]
        gi_ref[k] = total.astype(BF16)
    for i in range(1, n_dp):
        outgoing(i).wait_send()

    @pl.when(target != mp)
    def _():
        outgoing(0).wait_send()

    for copy in h_across + h_down:
        copy.wait_send()


def residual(n_dp, e_ref, a_ref, h_ref, qn_ref, b_ref, out_ref, up_ref, y):
    tok, rank = h_ref.shape[0], qn_ref.shape[1]
    rows = e_ref.shape[0]
    step = pl.program_id(0)

    @pl.when(step == 0)
    def _():
        high, low = split(-qn_ref[...].T)
        y[:rank] = high
        y[rank : 2 * rank] = high
        y[2 * rank : 3 * rank] = low
        y[3 * rank :] = h_ref[...]
        share = up_ref.shape[0]
        own = b_ref[pl.ds(pl.multiple_of(lax.axis_index("dp") * share, 16), share), :]
        x = jnp.concatenate([own, own[:, :rank]], axis=1)
        up_ref[...] = -dot(x, y[: 3 * rank, :])

    b = b_ref[pl.ds(pl.multiple_of(step * rows, 16), rows), :]
    x = jnp.concatenate([b, b[:, :rank], a_ref[...].T], axis=1)
    out_ref[...] = (e_ref[...].astype(F32) + dot(x, y[...])).astype(BF16)


def local(n_dp, n_mp, activations, grad_hidden, up_weight, error_feedback, query_previous):
    error = error_feedback[0]
    d, ff = error.shape
    tok, rank = activations.shape[0], query_previous.shape[1]
    chips = n_dp // CORES
    pr, tr = d // n_dp, ff // n_dp
    zr = pr // n_mp if pr % (8 * n_mp) == 0 else pr
    vmem = pl.BlockSpec(memory_space=pltpu.VMEM)
    hbm = pl.BlockSpec(memory_space=pl.ANY)
    dma = pltpu.SemaphoreType.DMA
    pairs = lambda n: [dma((n,)), dma((n,))]
    query_next, basis, input_blocks = pl.pallas_call(
        functools.partial(compress, n_dp, n_mp),
        out_shape=(
            jax.ShapeDtypeStruct((ff, rank), F32),
            jax.ShapeDtypeStruct((d, 2 * rank), BF16),
            jax.ShapeDtypeStruct((n_dp // n_mp, tok, pr), BF16),
        ),
        in_specs=[hbm, vmem, hbm, vmem, vmem, vmem],
        out_specs=(vmem, vmem, vmem),
        scratch_shapes=[
            pltpu.VMEM((d + tok, ff), BF16),
            pltpu.VMEM((ff, 2 * rank), BF16),
            pltpu.VMEM((d, rank), F32),
            pltpu.VMEM((2 * rank, d + tok), BF16),
            pltpu.VMEM((rank, 2 * rank), F32),
            pltpu.VMEM((pr, rank), F32),
            pltpu.VMEM((n_mp, zr, rank), F32),
            pltpu.VMEM((zr, rank), F32),
            pltpu.VMEM((chips, pr, rank), F32),
            pltpu.VMEM((chips, pr, rank), F32),
            pltpu.VMEM((chips, pr, rank), F32),
            pltpu.VMEM((chips, pr, rank), F32),
            pltpu.VMEM((ff, rank), F32),
            pltpu.VMEM((chips, tr, rank), F32),
            pltpu.VMEM((chips, tr, rank), F32),
            pltpu.VMEM((chips, tr, rank), F32),
            pltpu.VMEM((n_dp, tok, ff), BF16),
            pltpu.VMEM((n_dp, tok, pr), F32),
            pltpu.VMEM((n_dp, tok, pr), F32),
            dma((n_dp + 1,)),
        ]
        + pairs(chips) + pairs(chips) + pairs(n_mp) + pairs(n_mp) + pairs(chips) + pairs(chips)
        + pairs(chips) + pairs(chips) + pairs(chips) + pairs(chips) + pairs(chips) + pairs(chips) + pairs(n_dp),
        compiler_params=pltpu.CompilerParams(
            collective_id=0, has_side_effects=True, vmem_limit_bytes=48 << 20
        ),
        cost_estimate=pl.CostEstimate(flops=8 * d * ff * rank, bytes_accessed=4 * d * ff, transcendentals=0),
        name="compress",
    )(error, activations, grad_hidden, grad_hidden, query_previous, up_weight)
    grad_input = jnp.swapaxes(input_blocks, 0, 1).reshape(tok, d // n_mp)

    block = 256
    error_next, update = pl.pallas_call(
        functools.partial(residual, n_dp),
        out_shape=(
            jax.ShapeDtypeStruct((d, ff), BF16),
            jax.ShapeDtypeStruct((pr, ff), F32),
        ),
        grid=(d // block,),
        in_specs=[
            pl.BlockSpec((block, ff), lambda i: (i, 0)),
            pl.BlockSpec((tok, block), lambda i: (0, i)),
            pl.BlockSpec((tok, ff), lambda i: (0, 0)),
            pl.BlockSpec((ff, rank), lambda i: (0, 0)),
            pl.BlockSpec((d, 2 * rank), lambda i: (0, 0)),
        ],
        out_specs=(
            pl.BlockSpec((block, ff), lambda i: (i, 0)),
            pl.BlockSpec((pr, ff), lambda i: (0, 0)),
        ),
        scratch_shapes=[pltpu.VMEM((3 * rank + tok, ff), BF16)],
        compiler_params=pltpu.CompilerParams(vmem_limit_bytes=40 << 20),
        cost_estimate=pl.CostEstimate(flops=8 * d * ff * rank, bytes_accessed=4 * d * ff, transcendentals=0),
        name="residual",
    )(error, activations, grad_hidden, query_next, basis)
    return grad_input, error_next[None], update, query_next


def solution(mesh):
    n_dp, n_mp = mesh.shape["dp"], mesh.shape["mp"]
    in_specs = (P("dp", None), P("dp", "mp"), P("dp", "mp"), P("dp", None, "mp"), P("mp", None))
    out_specs = (P("dp", "mp"), P("dp", None, "mp"), P("dp", "mp"), P("mp", None))
    return jax.shard_map(
        functools.partial(local, n_dp, n_mp),
        mesh=mesh, in_specs=in_specs, out_specs=out_specs, check_vma=False,
    )
```

```python
import functools

import jax
import jax.numpy as jnp
from jax import lax
from jax.experimental import pallas as pl
from jax.experimental.pallas import tpu as pltpu
from jax.sharding import PartitionSpec as P

HIGHEST = lax.Precision.HIGHEST
MESH = pl.DeviceIdType.MESH
F32 = jnp.float32
BF16 = jnp.bfloat16
CORES = 2
PANEL = 16


def split(x):
    high = x.astype(BF16)
    return high, (x - high.astype(F32)).astype(BF16)


def dot(a, b, da=1, db=0, precision=None):
    return lax.dot_general(
        a, b, (((da,), (db,)), ((), ())), precision=precision, preferred_element_type=F32
    )


def halves(x):
    r = x.shape[1] // 2
    return x[:, :r] + x[:, r:]


def inverse_factor(gram, aug):
    r = gram.shape[0]
    rows = lax.broadcasted_iota(jnp.int32, (r, r), 0)
    cols = lax.broadcasted_iota(jnp.int32, (r, r), 1)
    aug[:, :r] = gram
    aug[:, r:] = jnp.where(rows == cols, 1.0, 0.0).astype(F32)
    prow = lax.broadcasted_iota(jnp.int32, (PANEL, 2 * r), 0)
    for start in range(0, r, PANEL):
        panel = aug[start : start + PANEL, :]
        for t in range(PANEL):
            j = start + t
            scale = lax.rsqrt(panel[t : t + 1, j : j + 1])
            row = panel[t : t + 1, :] * scale
            col = panel[:, j : j + 1] * scale
            panel = jnp.where(
                prow == t, row, jnp.where(prow > t, panel - col * row, panel)
            )
        aug[start : start + PANEL, :] = panel
        rest = start + PANEL
        if rest < r:
            change = dot(panel[:, :r], panel, 0, 0, HIGHEST)
            aug[rest:, :] = aug[rest:, :] - change[rest:, :]
    return aug[:, r:]


def compress(
    n_dp, n_mp, e_hbm, a_ref, h_hbm, h_ref, q_ref, qn_ref, b_ref, h_out,
    e, q2, p, pt2, aug, acc, zin, zfin, csend, crecv, xsend, xrecv,
    t, tcrecv, txsend, txrecv,
    e_sem, c_s, c_r, x_s, x_r, z_s, z_r, gz_s, gz_r, gx_s, gx_r, gc_s, gc_r,
    tc_s, tc_r, tx_s, tx_r, qx_s, qx_r, qc_s, qc_r,
):
    chips = n_dp // CORES
    me, mp = lax.axis_index("dp"), lax.axis_index("mp")
    chip, core = me // CORES, lax.rem(me, CORES)
    other = 1 - core
    partner = (chip * CORES + other, mp)
    d, rank = p.shape
    ff = t.shape[0]
    pr, tr = d // n_dp, ff // n_dp
    zr = pr // n_mp if pr % (8 * n_mp) == 0 else pr

    def chip_at(r):
        return lax.rem(chip + r, chips)

    def same_core(r):
        return (chip_at(r) * CORES + core, mp)

    def along(r):
        return (me, lax.rem(mp + r, n_mp))

    def rows(i, n):
        return pl.ds(pl.multiple_of(i * n, 8), n)

    def send(src, dst, s, r, to):
        return pltpu.make_async_remote_copy(
            src_ref=src, dst_ref=dst, send_sem=s, recv_sem=r, device_id=to, device_id_type=MESH
        )

    barrier = pltpu.get_barrier_semaphore()
    pl.semaphore_signal(barrier, inc=1, device_id=partner, device_id_type=MESH)
    for r in range(1, chips):
        pl.semaphore_signal(barrier, inc=1, device_id=same_core(r), device_id_type=MESH)
    for r in range(1, n_mp):
        pl.semaphore_signal(barrier, inc=1, device_id=along(r), device_id_type=MESH)

    order = [chip_at(r) * CORES + other for r in range(1, chips)] + [partner[0]]
    order += [chip_at(r) * CORES + core for r in range(1, chips)] + [me]
    loads = []
    for i, block in enumerate(order):
        at = pl.ds(pl.multiple_of(block * pr, 16), pr)
        copy = pltpu.make_async_copy(e_hbm.at[at, :], e.at[at, :], e_sem.at[i])
        copy.start()
        loads.append(copy)
    h_load = pltpu.make_async_copy(h_hbm, e.at[pl.ds(d, h_ref.shape[0]), :], e_sem.at[n_dp])
    h_load.start()

    h_out[...] = h_ref[...]
    q_high, q_low = split(q_ref[...])
    q2[:, :rank] = q_high
    q2[:, rank:] = q_low
    hq = halves(dot(h_ref[...], q2[...]))
    hq2 = jnp.concatenate(split(hq), axis=1)
    p[...] = halves(dot(a_ref[...], hq2, 0, 0))

    def project(i):
        loads[i].wait()
        block = order[i]
        at = pl.ds(pl.multiple_of(block * pr, 16), pr)
        return halves(dot(e[at, :], q2[...])) + p[rows(block, pr), :]

    pl.semaphore_wait(barrier, 1 + (chips - 1) + (n_mp - 1))
    core_copies = []
    for i in range(chips):
        csend[i] = project(i)
        copy = send(csend.at[i], crecv.at[i], c_s.at[i], c_r.at[i], partner)
        copy.start()
        core_copies.append(copy)
    x_copies = []
    for i in range(chips):
        value = project(chips + i)
        core_copies[i].wait_recv()
        value = value + crecv[i]
        if i < chips - 1:
            xsend[i] = value
            copy = send(xsend.at[i], xrecv.at[i], x_s.at[i], x_r.at[i], same_core(i + 1))
            copy.start()
            x_copies.append(copy)
        else:
            acc[...] = value
    h_load.wait()
    value = acc[...]
    for i, copy in enumerate(x_copies):
        copy.wait_recv()
        value = value + xrecv[i]
    acc[...] = value

    def part(i):
        return rows(i, zr) if zr < pr else pl.ds(0, pr)

    z_copies = []
    for r in range(1, n_mp):
        copy = send(
            acc.at[part(lax.rem(mp + r, n_mp)), :], zin.at[r - 1], z_s.at[r - 1], z_r.at[r - 1], along(r)
        )
        copy.start()
        z_copies.append(copy)
    value = acc[part(mp), :]
    for i, copy in enumerate(z_copies):
        copy.wait_recv()
        value = value + zin[i]
    mine = pl.ds(pl.multiple_of(me * pr, 8), pr)
    if zr < pr:
        zfin[...] = value
        here = pl.ds(pl.multiple_of(me * pr + mp * zr, 8), zr)
        p[here, :] = value
        gz = []
        for r in range(1, n_mp):
            copy = send(zfin, p.at[here, :], gz_s.at[r - 1], gz_r.at[r - 1], along(r))
            copy.start()
            gz.append(copy)
        for r in range(1, n_mp):
            gz[r - 1].wait_recv()
        z_copies += gz
    else:
        p[mine, :] = value

    def gather(ref, n, x_s, x_r, c_s, c_r, between=None):
        own = pl.ds(pl.multiple_of(me * n, 8), n)
        across, down = [], []
        for r in range(1, chips):
            copy = send(ref.at[own, :], ref.at[own, :], x_s.at[r - 1], x_r.at[r - 1], same_core(r))
            copy.start()
            across.append(copy)
        copy = send(ref.at[own, :], ref.at[own, :], c_s.at[chips - 1], c_r.at[chips - 1], partner)
        copy.start()
        down.append(copy)
        if between is not None:
            between()
        for r in range(1, chips):
            across[r - 1].wait_recv()
            block = lax.rem(chip + chips - r, chips) * CORES + core
            at = pl.ds(pl.multiple_of(block * n, 8), n)
            copy = send(ref.at[at, :], ref.at[at, :], c_s.at[r - 1], c_r.at[r - 1], partner)
            copy.start()
            down.append(copy)
        for copy in down:
            copy.wait_recv()
        return across + down

    started = core_copies + x_copies
    for copy in started:
        copy.wait_send()
    for copy in z_copies:
        copy.wait_send()
    for copy in gather(p, pr, gx_s, gx_r, gc_s, gc_r):
        copy.wait_send()

    pt = p[...].T
    high, low = split(pt)
    pt2[:rank, :d] = high
    pt2[rank:, :d] = low
    ap = dot(pt2[:, :d], a_ref[...], 1, 1)
    high, low = split(ap[:rank] + ap[rank:])
    pt2[:rank, d:] = high
    pt2[rank:, d:] = low
    width = 256

    def term(n, carry):
        at = pl.ds(pl.multiple_of(n * width, width), width)
        both = dot(pt2[...], e[:, at])
        t[at, :] = (both[:rank] + both[rank:]).T
        return carry

    lax.fori_loop(0, ff // width, term, 0)
    t_copies = []
    for i in range(chips):
        block = chip_at(i + 1) * CORES + other
        copy = send(t.at[rows(block, tr), :], tcrecv.at[i], tc_s.at[i], tc_r.at[i], partner)
        copy.start()
        t_copies.append(copy)
    gram = dot(pt, p[...], 1, 0, HIGHEST)
    tx_copies = []
    for i in range(chips):
        t_copies[i].wait_recv()
        value = t[rows(chip_at(i + 1) * CORES + core, tr), :] + tcrecv[i]
        txsend[i] = value
        if i < chips - 1:
            copy = send(txsend.at[i], txrecv.at[i], tx_s.at[i], tx_r.at[i], same_core(i + 1))
            copy.start()
            tx_copies.append(copy)
    inverse = inverse_factor(gram, aug)
    value = txsend[chips - 1]
    for i, copy in enumerate(tx_copies):
        copy.wait_recv()
        value = value + txrecv[i]
    for copy in t_copies + tx_copies:
        copy.wait_send()
    qn_ref[rows(me, tr), :] = dot(value, inverse, 1, 1, HIGHEST) / n_dp

    def basis():
        high, low = split(dot(p[...], aug[:, rank:], 1, 1, HIGHEST))
        b_ref[:, :rank] = high
        b_ref[:, rank:] = low

    for copy in gather(qn_ref, tr, qx_s, qx_r, qc_s, qc_r, basis):
        copy.wait_send()


def residual(n_dp, e_ref, a_ref, h_ref, qn_ref, b_ref, out_ref, up_ref, y):
    tok, rank = h_ref.shape[0], qn_ref.shape[1]
    rows = e_ref.shape[0]
    step = pl.program_id(0)

    @pl.when(step == 0)
    def _():
        high, low = split(-qn_ref[...].T)
        y[:rank] = high
        y[rank : 2 * rank] = high
        y[2 * rank : 3 * rank] = low
        y[3 * rank :] = h_ref[...]
        share = up_ref.shape[0]
        own = b_ref[pl.ds(pl.multiple_of(lax.axis_index("dp") * share, 16), share), :]
        x = jnp.concatenate([own, own[:, :rank]], axis=1)
        up_ref[...] = -dot(x, y[: 3 * rank, :])

    b = b_ref[pl.ds(pl.multiple_of(step * rows, 16), rows), :]
    x = jnp.concatenate([b, b[:, :rank], a_ref[...].T], axis=1)
    out_ref[...] = (e_ref[...].astype(F32) + dot(x, y[...])).astype(BF16)


def local(n_dp, n_mp, activations, grad_hidden, up_weight, error_feedback, query_previous):
    error = error_feedback[0]
    d, ff = error.shape
    tok, rank = activations.shape[0], query_previous.shape[1]
    weight = lax.all_gather(up_weight, "dp", axis=0, tiled=True)
    chips = n_dp // CORES
    pr, tr = d // n_dp, ff // n_dp
    zr = pr // n_mp if pr % (8 * n_mp) == 0 else pr
    vmem = pl.BlockSpec(memory_space=pltpu.VMEM)
    hbm = pl.BlockSpec(memory_space=pl.ANY)
    dma = pltpu.SemaphoreType.DMA
    pairs = lambda n: [dma((n,)), dma((n,))]
    query_next, basis, hidden = pl.pallas_call(
        functools.partial(compress, n_dp, n_mp),
        out_shape=(
            jax.ShapeDtypeStruct((ff, rank), F32),
            jax.ShapeDtypeStruct((d, 2 * rank), BF16),
            jax.ShapeDtypeStruct((tok, ff), BF16),
        ),
        in_specs=[hbm, vmem, hbm, vmem, vmem],
        out_specs=(vmem, vmem, vmem),
        scratch_shapes=[
            pltpu.VMEM((d + tok, ff), BF16),
            pltpu.VMEM((ff, 2 * rank), BF16),
            pltpu.VMEM((d, rank), F32),
            pltpu.VMEM((2 * rank, d + tok), BF16),
            pltpu.VMEM((rank, 2 * rank), F32),
            pltpu.VMEM((pr, rank), F32),
            pltpu.VMEM((n_mp, zr, rank), F32),
            pltpu.VMEM((zr, rank), F32),
            pltpu.VMEM((chips, pr, rank), F32),
            pltpu.VMEM((chips, pr, rank), F32),
            pltpu.VMEM((chips, pr, rank), F32),
            pltpu.VMEM((chips, pr, rank), F32),
            pltpu.VMEM((ff, rank), F32),
            pltpu.VMEM((chips, tr, rank), F32),
            pltpu.VMEM((chips, tr, rank), F32),
            pltpu.VMEM((chips, tr, rank), F32),
            dma((n_dp + 1,)),
        ]
        + pairs(chips) + pairs(chips) + pairs(n_mp) + pairs(n_mp) + pairs(chips) + pairs(chips)
        + pairs(chips) + pairs(chips) + pairs(chips) + pairs(chips),
        compiler_params=pltpu.CompilerParams(
            collective_id=0, has_side_effects=True, vmem_limit_bytes=48 << 20
        ),
        cost_estimate=pl.CostEstimate(flops=64 * d * ff * rank, bytes_accessed=48 * d * ff, transcendentals=0),
        name="compress",
    )(error, activations, grad_hidden, grad_hidden, query_previous)
    partial_input = dot(hidden, weight, 1, 1)
    grad_input = lax.psum_scatter(partial_input, "mp", scatter_dimension=1, tiled=True).astype(BF16)

    block = 256
    error_next, update = pl.pallas_call(
        functools.partial(residual, n_dp),
        out_shape=(
            jax.ShapeDtypeStruct((d, ff), BF16),
            jax.ShapeDtypeStruct((pr, ff), F32),
        ),
        grid=(d // block,),
        in_specs=[
            pl.BlockSpec((block, ff), lambda i: (i, 0)),
            pl.BlockSpec((tok, block), lambda i: (0, i)),
            pl.BlockSpec((tok, ff), lambda i: (0, 0)),
            pl.BlockSpec((ff, rank), lambda i: (0, 0)),
            pl.BlockSpec((d, 2 * rank), lambda i: (0, 0)),
        ],
        out_specs=(
            pl.BlockSpec((block, ff), lambda i: (i, 0)),
            pl.BlockSpec((pr, ff), lambda i: (0, 0)),
        ),
        scratch_shapes=[pltpu.VMEM((3 * rank + tok, ff), BF16)],
        compiler_params=pltpu.CompilerParams(vmem_limit_bytes=40 << 20),
        cost_estimate=pl.CostEstimate(flops=8 * d * ff * rank, bytes_accessed=4 * d * ff, transcendentals=0),
        name="residual",
    )(error, activations, grad_hidden, query_next, basis)
    return grad_input, error_next[None], update, query_next


def solution(mesh):
    n_dp, n_mp = mesh.shape["dp"], mesh.shape["mp"]
    in_specs = (P("dp", None), P("dp", "mp"), P("dp", "mp"), P("dp", None, "mp"), P("mp", None))
    out_specs = (P("dp", "mp"), P("dp", None, "mp"), P("dp", "mp"), P("mp", None))
    return jax.shard_map(
        functools.partial(local, n_dp, n_mp),
        mesh=mesh, in_specs=in_specs, out_specs=out_specs, check_vma=False,
    )
```
